32 devices in a mesh: row: 8 (over z, y), col: 4 (over x, core).
Axes of the slice: x: 2, y: 2, z: 4, core: 2. Of those that a mesh axis runs over, the one named last changes fastest.
Arguments:
- pair: bfloat16 [768, 768, 128], P('row', 'col'), may hold values from -6 to 6
- chain_lengths: int32 [8], replicated, may hold values from 1 to 96, 576 in all
- gains: float32 [2, 2, 128], replicated, may hold values from 0.1 to 1.9
- biases: float32 [2, 2, 128], replicated, may hold values from -3 to 3
- w_in: bfloat16 [2, 128, 640], replicated, may hold values from -0.5 to 0.5
- w_out: bfloat16 [2, 128, 128], replicated, may hold values from -0.5 to 0.5
Outputs:
- pair_out: bfloat16 [768, 768, 128], P('row', 'col')
The draws below stay inside these ranges and needn't reach their ends.
Inputs may be any that keep to these rules, and one draw needn't show every extreme that they name: Chain k occupies positions k * 96 to (k + 1) * 96 - 1 and its live residues are the first chain_lengths[k] of them; the lengths sum to 576 and one of them equals 96.
All inputs are finite; a program needn't handle non-finite values.
Results may differ from the reference program's by a relative error of at most 0.0054.
Values may be sent and summed in bfloat16 or wider, within the bound.
A program may use at most 128 MiB of HBM per device.

```python
import math
import jax
import jax.numpy as jnp
import numpy as np
from jax import lax

C = 128
N = 768
NCHAIN = 8


def level_of(stream_key, shape, shards, least, high):
    def one(position, blocks):
        heights = jax.random.uniform(jax.random.fold_in(jax.random.fold_in(stream_key, 6), position), (blocks,), jnp.float32, least / len(shards), high / len(shards))
        return jnp.repeat(jnp.exp(heights), shape[position] // blocks).reshape((-1,) + (1,) * (len(shape) - position - 1))

    level = one(*shards[0])
    for cut in shards[1:]:
        level = level * one(*cut)
    return level


def profile(amount, total, bound, lean):
    weights = [(1 << 20) // math.isqrt(rank ** lean) + 1 for rank in range(2, amount + 1)]
    spare, holding = total - bound - (amount - 1), [1] * (amount - 1)
    while spare > 0:
        free = [i for i in range(amount - 1) if holding[i] < bound]
        mass, budget = sum([weights[i] for i in free]), spare
        for i in free:
            more = min(bound - holding[i], max(1, budget * weights[i] // mass), spare)
            holding[i] = holding[i] + more
            spare = spare - more
    return np.array([bound] + holding)


def uneven_parts(rng, count, total, most, skew):
    if count == 2:
        one = jax.random.randint(rng, (), max(1, total - most), min(most, total - 1) + 1)
        return jnp.stack([one, total - one])
    sizes = jnp.asarray(profile(count, total, most, skew), jnp.int32)
    pairs = (count - 1) // 2
    giver, sink = sizes[1:1 + 2 * pairs:2], sizes[2:2 + 2 * pairs:2]
    slack = jnp.minimum(giver - 1, most - sink)
    passed = jax.random.randint(jax.random.fold_in(rng, 1), (pairs,), 0, 1 << 20) % (slack + 1)
    sizes = sizes.at[1:1 + 2 * pairs:2].set(giver - passed).at[2:2 + 2 * pairs:2].set(sink + passed)
    return sizes[jax.random.permutation(jax.random.fold_in(rng, 2), count)]


def bell_draw(stream_key, shape, deviation, bound, cuts=(), held_as=jnp.bfloat16):
    array = deviation * jax.random.normal(stream_key, shape, jnp.float32)
    if cuts:
        array = array * level_of(stream_key, shape, cuts, -0.22, 0.18)
    return jnp.clip(array, -bound, bound).astype(held_as)


def setup_inputs(seed: int = 0) -> dict:
    key_of = jax.random.split(jax.random.key(seed), 7)
    return {
        "pair": bell_draw(key_of[0], (N, N, C), 1.0, 6.0, ((0, 8), (1, 4))),
        "chain_lengths": uneven_parts(key_of[1], NCHAIN, 3 * N // 4, N // NCHAIN, 1).astype(jnp.int32),
        "gains": jnp.clip(1.0 + 0.18 * jax.random.normal(key_of[2], (2, 2, C), jnp.float32), 0.1, 1.9),
        "biases": bell_draw(key_of[3], (2, 2, C), 0.5, 3.0, (), jnp.float32),
        "w_in": bell_draw(key_of[4], (2, C, 5 * C), C ** -0.5, 0.5),
        "w_out": bell_draw(key_of[5], (2, C, C), C ** -0.5, 0.5),
    }


def layer_norm(values, gain_vec, bias_vec):
    wide = values.astype(jnp.float32)
    average = lax.optimization_barrier(jnp.mean(wide, axis=-1, keepdims=True))
    centred = wide - average
    variance = lax.optimization_barrier(jnp.mean(centred * centred, axis=-1, keepdims=True))
    return centred * jax.lax.rsqrt(variance + 1e-05) * gain_vec + bias_vec

def live_mask(chain_lengths):
    slot_size = N // NCHAIN
    positions = jnp.arange(N, dtype=jnp.int32)
    live_length = chain_lengths[positions // slot_size]
    return (positions % slot_size < live_length).astype(jnp.float32)

def one_update(state, pmask, gain_pair, bias_pair, weights_in, weights_out, incoming):
    channels = state.shape[-1]
    normed = layer_norm(state, gain_pair[0], bias_pair[0]).astype(jnp.bfloat16)
    flat = normed.reshape(N * N, channels)

    def project(column_block):
        block = weights_in[:, column_block * channels:(column_block + 1) * channels]
        return jnp.dot(flat, block, preferred_element_type=jnp.float32).reshape(N, N, channels)
    left_edges = (pmask * jax.nn.sigmoid(project(1)) * project(0)).astype(jnp.bfloat16)
    right_edges = (pmask * jax.nn.sigmoid(project(3)) * project(2)).astype(jnp.bfloat16)
    left_wide = left_edges.astype(jnp.float32)
    right_wide = right_edges.astype(jnp.float32)
    if incoming:
        products = jnp.einsum('kic,kjc->ijc', left_wide, right_wide)
    else:
        products = jnp.einsum('ikc,jkc->ijc', left_wide, right_wide)
    products = products.astype(jnp.bfloat16)
    normed_out = layer_norm(products, gain_pair[1], bias_pair[1]).astype(jnp.bfloat16)
    mixed = jnp.dot(normed_out.reshape(N * N, channels), weights_out, preferred_element_type=jnp.float32).reshape(N, N, channels)
    gate_vals = jax.nn.sigmoid(project(4))
    return (state.astype(jnp.float32) + gate_vals * mixed).astype(jnp.bfloat16)

def reference(pair, chain_lengths, gains, biases, w_in, w_out):
    live = live_mask(chain_lengths)
    pmask = (live[:, None] * live[None, :])[:, :, None]
    state = pair
    for update_index in range(2):
        state = one_update(state, pmask, gains[update_index], biases[update_index], w_in[update_index], w_out[update_index], update_index == 1)
    return state
```

```python
import functools

import jax
import jax.numpy as jnp
from jax import lax
from jax.experimental import pallas as pl
from jax.experimental.pallas import tpu as pltpu
from jax.sharding import PartitionSpec as P

LANES = 128
HALF = LANES // 2


def layer_norm(values, gain_vec, bias_vec, axis_pos):
    wide = values.astype(jnp.float32)
    average = jnp.mean(wide, axis=axis_pos, keepdims=True)
    centred = wide - average
    variance = jnp.mean(centred * centred, axis=axis_pos, keepdims=True)
    return centred * jax.lax.rsqrt(variance + 1e-05) * gain_vec + bias_vec


def live_values(global_index, chain_lengths, total):
    n_chain = chain_lengths.shape[0]
    slot_size = total // n_chain
    chain_index = global_index // slot_size
    offset = global_index % slot_size
    matches = chain_index[:, None] == jnp.arange(n_chain, dtype=jnp.int32)[None, :]
    live_length = jnp.sum(jnp.where(matches, chain_lengths[None, :], 0), axis=1)
    return (offset < live_length).astype(jnp.float32)


def segments(start, length, tile_cols, n_col):
    runs, at = [], start
    while at < start + length:
        block, inside = divmod(at, tile_cols)
        if inside < LANES:
            stop, packed = block * tile_cols + LANES, block * LANES + inside
        else:
            stop, packed = (block + 1) * tile_cols, n_col * LANES + block * HALF + inside - LANES
        stop = min(stop, start + length)
        runs.append((at - start, packed, stop - at))
        at = stop
    return runs


def join(first, second, upper):
    lanes = slice(HALF, LANES) if upper else slice(0, HALF)
    return jnp.concatenate([first[:, lanes], second[:, lanes]], axis=1)


def triangle_kernel(geometry, incoming, left_ref, right_ref, out_ref, left, right, tri):
    n_row, n_col, rows, cols = geometry
    half = rows // 2

    def unpack(source, target, packed_rows):
        for r in range(n_row):
            if packed_rows:
                runs = segments(r * rows, rows, cols, n_col)
            else:
                runs = [(0, r * rows, rows)]

            def put(offset, block, lane_at):
                size = block.shape[0]
                for begin, packed, length in runs:
                    lo, hi = max(begin, offset), min(begin + length, offset + size)
                    if lo < hi:
                        target[packed + lo - begin:packed + hi - begin, lane_at:lane_at + LANES] = (
                            block[lo - offset:hi - offset]
                        )

            for s in range(n_col):
                put(0, source[r, s, 0, :rows, :], s * LANES)
            for p in range(n_col // 2):
                first = source[r, 2 * p, 0, rows:, :]
                second = source[r, 2 * p + 1, 0, rows:, :]
                lane_at = (n_col + p) * LANES
                put(0, join(first, second, False), lane_at)
                put(half, join(first, second, True), lane_at)

    unpack(left_ref, left, False)
    unpack(right_ref, right, not incoming)
    contract = ((0,), (0,)) if incoming else ((1,), (1,))
    tri[...] = lax.dot_general(
        left[...], right[...], (contract, ((), ())), preferred_element_type=jnp.float32
    ).astype(tri.dtype)

    for r in range(n_row):
        if incoming:
            runs = segments(r * rows, rows, cols, n_col)
        else:
            runs = [(0, r * rows, rows)]

        def get(offset, size, lane_at):
            parts = []
            for begin, packed, length in runs:
                lo, hi = max(begin, offset), min(begin + length, offset + size)
                if lo < hi:
                    parts.append(
                        tri[packed + lo - begin:packed + hi - begin, lane_at:lane_at + LANES]
                    )
            return parts[0] if len(parts) == 1 else jnp.concatenate(parts, axis=0)

        for s in range(n_col):
            out_ref[r, s, 0, :rows, :] = get(0, rows, s * LANES)
        for p in range(n_col // 2):
            lane_at = (n_col + p) * LANES
            above, below = get(0, half, lane_at), get(half, half, lane_at)
            out_ref[r, 2 * p, 0, rows:, :] = join(above, below, False)
            out_ref[r, 2 * p + 1, 0, rows:, :] = join(above, below, True)


def triangle(left, right, geometry, incoming):
    n_row, n_col, rows, cols = geometry
    owned, packed, lanes = left.shape[0] // (n_row * n_col), left.shape[1], left.shape[2]
    total = n_row * rows
    shape = (n_row, n_col, owned, packed, lanes)
    spec = pl.BlockSpec((n_row, n_col, 1, packed, lanes), lambda c: (0, 0, c, 0, 0))
    out = pl.pallas_call(
        functools.partial(triangle_kernel, geometry, incoming),
        grid=(owned,),
        in_specs=[spec, spec],
        out_specs=spec,
        out_shape=jax.ShapeDtypeStruct(shape, jnp.bfloat16),
        scratch_shapes=[pltpu.VMEM((total, total), jnp.bfloat16)] * 3,
        cost_estimate=pl.CostEstimate(
            flops=2 * owned * total**3, bytes_accessed=6 * left.size, transcendentals=0
        ),
        compiler_params=pltpu.CompilerParams(vmem_limit_bytes=48 * 2**20),
        name="triangle_in" if incoming else "triangle_out",
    )(left.reshape(shape), right.reshape(shape))
    return out.reshape(left.shape)


def pack_tile(tile):
    rows, _, channels = tile.shape
    tail = tile[:, LANES:].reshape(2, rows // 2, HALF, channels).transpose(1, 0, 2, 3)
    return jnp.concatenate([tile[:, :LANES], tail.reshape(rows // 2, LANES, channels)], axis=0)


def unpack_tile(packed, rows):
    channels = packed.shape[2]
    tail = packed[rows:].reshape(rows // 2, 2, HALF, channels).transpose(1, 0, 2, 3)
    return jnp.concatenate([packed[:rows], tail.reshape(rows, HALF, channels)], axis=1)


def packed_body(pair, chain_lengths, gains, biases, w_in, w_out):
    tile_rows, tile_cols, channels = pair.shape
    n_row = lax.axis_size("row")
    n_col = lax.axis_size("col")
    geometry = (n_row, n_col, tile_rows, tile_cols)
    total = n_row * tile_rows
    row_index = lax.axis_index("row") * tile_rows + jnp.arange(tile_rows, dtype=jnp.int32)
    col_index = lax.axis_index("col") * tile_cols + jnp.arange(tile_cols, dtype=jnp.int32)
    pmask = (
        live_values(row_index, chain_lengths, total)[:, None]
        * live_values(col_index, chain_lengths, total)[None, :]
    )
    pmask = pack_tile(pmask[:, :, None])[:, :, 0]

    def exchange(block):
        return lax.all_to_all(block, ("row", "col"), split_axis=0, concat_axis=0, tiled=True)

    state = pack_tile(pair)
    for update_index in range(2):
        weights_in = w_in[update_index]
        normed = layer_norm(state, gains[update_index, 0], biases[update_index, 0], 2).astype(
            jnp.bfloat16
        )

        def project_first(column_block):
            block = weights_in[:, column_block * channels : (column_block + 1) * channels]
            return jnp.einsum("ijc,cd->dij", normed, block, preferred_element_type=jnp.float32)

        left_edges = (pmask[None] * jax.nn.sigmoid(project_first(1)) * project_first(0)).astype(
            jnp.bfloat16
        )
        right_edges = (pmask[None] * jax.nn.sigmoid(project_first(3)) * project_first(2)).astype(
            jnp.bfloat16
        )
        products = triangle(
            exchange(left_edges), exchange(right_edges), geometry, update_index == 1
        )
        returned = exchange(products)
        gain_out = gains[update_index, 1]
        bias_out = biases[update_index, 1]
        normed_out = layer_norm(
            returned, gain_out[:, None, None], bias_out[:, None, None], 0
        ).astype(jnp.bfloat16)
        mixed = jnp.einsum(
            "cij,cd->ijd", normed_out, w_out[update_index], preferred_element_type=jnp.float32
        )
        gate_vals = jax.nn.sigmoid(
            jnp.einsum(
                "ijc,cd->ijd",
                normed,
                weights_in[:, 4 * channels : 5 * channels],
                preferred_element_type=jnp.float32,
            )
        )
        state = (state.astype(jnp.float32) + gate_vals * mixed).astype(jnp.bfloat16)
    return unpack_tile(state, tile_rows)


def body(pair, chain_lengths, gains, biases, w_in, w_out):
    tile_rows, tile_cols, channels = pair.shape
    n_row = lax.axis_size("row")
    n_col = lax.axis_size("col")
    if tile_cols == LANES + HALF and tile_rows % 32 == 0 and tile_cols % tile_rows == 0 and n_col % 2 == 0:
        return packed_body(pair, chain_lengths, gains, biases, w_in, w_out)
    owned_count = channels // (n_row * n_col)
    total = n_row * tile_rows
    row_index = lax.axis_index("row") * tile_rows + jnp.arange(tile_rows, dtype=jnp.int32)
    col_index = lax.axis_index("col") * tile_cols + jnp.arange(tile_cols, dtype=jnp.int32)
    pmask = (
        live_values(row_index, chain_lengths, total)[:, None]
        * live_values(col_index, chain_lengths, total)[None, :]
    )

    def return_products(products):
        split = products.reshape(owned_count, n_row, tile_rows, n_col, tile_cols)
        ordered = split.transpose(1, 3, 0, 2, 4).reshape(channels, tile_rows, tile_cols)
        return lax.all_to_all(ordered, ("row", "col"), split_axis=0, concat_axis=0, tiled=True)

    state = pair
    for update_index in range(2):
        weights_in = w_in[update_index]
        normed = layer_norm(state, gains[update_index, 0], biases[update_index, 0], 2).astype(
            jnp.bfloat16
        )

        def project_first(column_block):
            block = weights_in[:, column_block * channels : (column_block + 1) * channels]
            return jnp.einsum("ijc,cd->dij", normed, block, preferred_element_type=jnp.float32)

        left_edges = (pmask[None] * jax.nn.sigmoid(project_first(1)) * project_first(0)).astype(
            jnp.bfloat16
        )
        right_edges = (pmask[None] * jax.nn.sigmoid(project_first(3)) * project_first(2)).astype(
            jnp.bfloat16
        )

        def squared(block):
            split = block.reshape(owned_count, n_row, n_col, tile_rows, tile_cols)
            return split.transpose(0, 1, 3, 2, 4).reshape(
                owned_count, n_row * tile_rows, n_col * tile_cols
            )

        left_full = squared(
            lax.all_to_all(
                left_edges[:, None], ("row", "col"), split_axis=0, concat_axis=1, tiled=True
            )
        )
        right_full = squared(
            lax.all_to_all(
                right_edges[:, None], ("row", "col"), split_axis=0, concat_axis=1, tiled=True
            )
        )
        equation = "cki,ckj->cij" if update_index == 1 else "cik,cjk->cij"
        products = jnp.einsum(
            equation, left_full, right_full, preferred_element_type=jnp.float32
        )
        returned = return_products(products.astype(jnp.bfloat16))
        gain_out = gains[update_index, 1]
        bias_out = biases[update_index, 1]
        normed_out = layer_norm(
            returned, gain_out[:, None, None], bias_out[:, None, None], 0
        ).astype(jnp.bfloat16)
        mixed = jnp.einsum(
            "cij,cd->ijd", normed_out, w_out[update_index], preferred_element_type=jnp.float32
        )
        gate_vals = jax.nn.sigmoid(
            jnp.dot(
                normed.reshape(tile_rows * tile_cols, channels),
                weights_in[:, 4 * channels : 5 * channels],
                preferred_element_type=jnp.float32,
            ).reshape(tile_rows, tile_cols, channels)
        )
        state = (state.astype(jnp.float32) + gate_vals * mixed).astype(jnp.bfloat16)
    return state


def solution(mesh):
    placed = (P("row", "col", None), P(), P(), P(), P(), P())
    return jax.shard_map(
        body, mesh=mesh, in_specs=placed, out_specs=P("row", "col", None), check_vma=False
    )
```

```python
import functools

import jax
import jax.numpy as jnp
from jax import lax
from jax.experimental import pallas as pl
from jax.experimental.pallas import tpu as pltpu
from jax.sharding import PartitionSpec as P

LANES = 128
HALF = LANES // 2


def layer_norm(values, gain_vec, bias_vec, axis_pos):
    wide = values.astype(jnp.float32)
    average = jnp.mean(wide, axis=axis_pos, keepdims=True)
    centred = wide - average
    variance = jnp.mean(centred * centred, axis=axis_pos, keepdims=True)
    return centred * jax.lax.rsqrt(variance + 1e-05) * gain_vec + bias_vec


def live_values(global_index, chain_lengths, total):
    n_chain = chain_lengths.shape[0]
    slot_size = total // n_chain
    chain_index = global_index // slot_size
    offset = global_index % slot_size
    matches = chain_index[:, None] == jnp.arange(n_chain, dtype=jnp.int32)[None, :]
    live_length = jnp.sum(jnp.where(matches, chain_lengths[None, :], 0), axis=1)
    return (offset < live_length).astype(jnp.float32)


def segments(start, length, tile_cols, n_col):
    runs, at = [], start
    while at < start + length:
        block, inside = divmod(at, tile_cols)
        if inside < LANES:
            stop, packed = block * tile_cols + LANES, block * LANES + inside
        else:
            stop, packed = (block + 1) * tile_cols, n_col * LANES + block * HALF + inside - LANES
        stop = min(stop, start + length)
        runs.append((at - start, packed, stop - at))
        at = stop
    return runs


def join(first, second, upper):
    lanes = slice(HALF, LANES) if upper else slice(0, HALF)
    return jnp.concatenate([first[:, lanes], second[:, lanes]], axis=1)


def triangle_kernel(geometry, incoming, *refs):
    n_row, n_col, rows, cols, first_rows = geometry
    half = rows // 2
    left_parts, right_parts, out_parts = refs[0:2], refs[2:4], refs[4:6]
    left, right, tri = refs[6:]
    rest = rows - first_rows

    def runs_of(r, packed_rows):
        return segments(r * rows, rows, cols, n_col) if packed_rows else [(0, r * rows, rows)]

    def unpack(parts, target, packed_rows):
        first, second = parts
        for r in range(n_row):
            runs = runs_of(r, packed_rows)

            def put(offset, block, lane_at):
                size = block.shape[0]
                for begin, packed, length in runs:
                    lo, hi = max(begin, offset), min(begin + length, offset + size)
                    if lo < hi:
                        target[packed + lo - begin:packed + hi - begin, lane_at:lane_at + LANES] = (
                            block[lo - offset:hi - offset]
                        )

            for s in range(n_col):
                put(0, first[r, s, 0], s * LANES)
                put(first_rows, second[r, s, 0, :rest, :], s * LANES)
            for p in range(n_col // 2):
                even = second[r, 2 * p, 0, rest:, :]
                odd = second[r, 2 * p + 1, 0, rest:, :]
                lane_at = (n_col + p) * LANES
                put(0, join(even, odd, False), lane_at)
                put(half, join(even, odd, True), lane_at)

    unpack(left_parts, left, False)
    unpack(right_parts, right, not incoming)
    contract = ((0,), (0,)) if incoming else ((1,), (1,))
    tri[...] = lax.dot_general(
        left[...], right[...], (contract, ((), ())), preferred_element_type=jnp.float32
    ).astype(tri.dtype)

    first, second = out_parts
    for r in range(n_row):
        runs = runs_of(r, incoming)

        def get(offset, size, lane_at):
            pieces = []
            for begin, packed, length in runs:
                lo, hi = max(begin, offset), min(begin + length, offset + size)
                if lo < hi:
                    pieces.append(
                        tri[packed + lo - begin:packed + hi - begin, lane_at:lane_at + LANES]
                    )
            return pieces[0] if len(pieces) == 1 else jnp.concatenate(pieces, axis=0)

        for s in range(n_col):
            first[r, s, 0] = get(0, first_rows, s * LANES)
            second[r, s, 0, :rest, :] = get(first_rows, rest, s * LANES)
        for p in range(n_col // 2):
            lane_at = (n_col + p) * LANES
            above, below = get(0, half, lane_at), get(half, half, lane_at)
            second[r, 2 * p, 0, rest:, :] = join(above, below, False)
            second[r, 2 * p + 1, 0, rest:, :] = join(above, below, True)


def triangle(left, right, geometry, incoming):
    n_row, n_col, rows = geometry[:3]
    owned = left[0].shape[0] // (n_row * n_col)
    total = n_row * rows
    shapes = [(n_row, n_col, owned) + part.shape[1:] for part in left]
    specs = [
        pl.BlockSpec((n_row, n_col, 1) + shape[3:], lambda c: (0, 0, c, 0, 0)) for shape in shapes
    ]
    outs = pl.pallas_call(
        functools.partial(triangle_kernel, geometry, incoming),
        grid=(owned,),
        in_specs=specs * 2,
        out_specs=specs,
        out_shape=[jax.ShapeDtypeStruct(shape, jnp.bfloat16) for shape in shapes],
        scratch_shapes=[pltpu.VMEM((total, total), jnp.bfloat16)] * 3,
        cost_estimate=pl.CostEstimate(
            flops=2 * owned * total**3,
            bytes_accessed=6 * sum(part.size for part in left),
            transcendentals=0,
        ),
        compiler_params=pltpu.CompilerParams(vmem_limit_bytes=48 * 2**20),
        name="triangle_in" if incoming else "triangle_out",
    )(*[part.reshape(shape) for part, shape in zip(left, shapes)],
      *[part.reshape(shape) for part, shape in zip(right, shapes)])
    return [out.reshape(part.shape) for out, part in zip(outs, left)]


def pack_tile(tile):
    rows, _, channels = tile.shape
    tail = tile[:, LANES:].reshape(2, rows // 2, HALF, channels).transpose(1, 0, 2, 3)
    return jnp.concatenate([tile[:, :LANES], tail.reshape(rows // 2, LANES, channels)], axis=0)


def unpack_tile(packed, rows):
    channels = packed.shape[2]
    tail = packed[rows:].reshape(rows // 2, 2, HALF, channels).transpose(1, 0, 2, 3)
    return jnp.concatenate([packed[:rows], tail.reshape(rows, HALF, channels)], axis=1)


def packed_body(pair, chain_lengths, gains, biases, w_in, w_out):
    tile_rows, tile_cols, channels = pair.shape
    n_row = lax.axis_size("row")
    n_col = lax.axis_size("col")
    first_rows = tile_rows - 16
    geometry = (n_row, n_col, tile_rows, tile_cols, first_rows)
    total = n_row * tile_rows
    row_index = lax.axis_index("row") * tile_rows + jnp.arange(tile_rows, dtype=jnp.int32)
    col_index = lax.axis_index("col") * tile_cols + jnp.arange(tile_cols, dtype=jnp.int32)
    pmask = (
        live_values(row_index, chain_lengths, total)[:, None]
        * live_values(col_index, chain_lengths, total)[None, :]
    )
    pmask = pack_tile(pmask[:, :, None])[:, :, 0]
    masks = [pmask[:first_rows], pmask[first_rows:]]

    def exchange(block):
        return lax.all_to_all(block, ("row", "col"), split_axis=0, concat_axis=0, tiled=True)

    def factor(normed, weights_in, column_block, mask):
        def project(at):
            block = weights_in[:, at * channels : (at + 1) * channels]
            return jnp.einsum("ijc,cd->dij", normed, block, preferred_element_type=jnp.float32)

        gate = jax.nn.sigmoid(project(column_block + 1))
        return (mask[None] * gate * project(column_block)).astype(jnp.bfloat16)

    states = [
        pair[:first_rows, :LANES],
        jnp.concatenate(
            [
                pair[first_rows:, :LANES],
                pair[:, LANES:].reshape(2, tile_rows // 2, HALF, channels)
                .transpose(1, 0, 2, 3)
                .reshape(tile_rows // 2, LANES, channels),
            ],
            axis=0,
        ),
    ]
    for update_index in range(2):
        weights_in = w_in[update_index]
        gain_in, gain_out = gains[update_index, 0], gains[update_index, 1]
        bias_in, bias_out = biases[update_index, 0], biases[update_index, 1]
        normed = [layer_norm(state, gain_in, bias_in, 2).astype(jnp.bfloat16) for state in states]
        left = [exchange(factor(n, weights_in, 0, m)) for n, m in zip(normed, masks)]
        right = [exchange(factor(n, weights_in, 2, m)) for n, m in zip(normed, masks)]
        products = triangle(left, right, geometry, update_index == 1)
        later = []
        for state, normed_part, part in zip(states, normed, products):
            returned = exchange(part)
            normed_out = layer_norm(
                returned, gain_out[:, None, None], bias_out[:, None, None], 0
            ).astype(jnp.bfloat16)
            mixed = jnp.einsum(
                "cij,cd->ijd", normed_out, w_out[update_index], preferred_element_type=jnp.float32
            )
            gate_vals = jax.nn.sigmoid(
                jnp.einsum(
                    "ijc,cd->ijd",
                    normed_part,
                    weights_in[:, 4 * channels : 5 * channels],
                    preferred_element_type=jnp.float32,
                )
            )
            later.append((state.astype(jnp.float32) + gate_vals * mixed).astype(jnp.bfloat16))
        states = later
    return unpack_tile(jnp.concatenate(states, axis=0), tile_rows)


def body(pair, chain_lengths, gains, biases, w_in, w_out):
    tile_rows, tile_cols, channels = pair.shape
    n_row = lax.axis_size("row")
    n_col = lax.axis_size("col")
    if tile_cols == LANES + HALF and tile_rows % 32 == 0 and tile_cols % tile_rows == 0 and n_col % 2 == 0:
        return packed_body(pair, chain_lengths, gains, biases, w_in, w_out)
    owned_count = channels // (n_row * n_col)
    total = n_row * tile_rows
    row_index = lax.axis_index("row") * tile_rows + jnp.arange(tile_rows, dtype=jnp.int32)
    col_index = lax.axis_index("col") * tile_cols + jnp.arange(tile_cols, dtype=jnp.int32)
    pmask = (
        live_values(row_index, chain_lengths, total)[:, None]
        * live_values(col_index, chain_lengths, total)[None, :]
    )

    def return_products(products):
        split = products.reshape(owned_count, n_row, tile_rows, n_col, tile_cols)
        ordered = split.transpose(1, 3, 0, 2, 4).reshape(channels, tile_rows, tile_cols)
        return lax.all_to_all(ordered, ("row", "col"), split_axis=0, concat_axis=0, tiled=True)

    state = pair
    for update_index in range(2):
        weights_in = w_in[update_index]
        normed = layer_norm(state, gains[update_index, 0], biases[update_index, 0], 2).astype(
            jnp.bfloat16
        )

        def project_first(column_block):
            block = weights_in[:, column_block * channels : (column_block + 1) * channels]
            return jnp.einsum("ijc,cd->dij", normed, block, preferred_element_type=jnp.float32)

        left_edges = (pmask[None] * jax.nn.sigmoid(project_first(1)) * project_first(0)).astype(
            jnp.bfloat16
        )
        right_edges = (pmask[None] * jax.nn.sigmoid(project_first(3)) * project_first(2)).astype(
            jnp.bfloat16
        )

        def squared(block):
            split = block.reshape(owned_count, n_row, n_col, tile_rows, tile_cols)
            return split.transpose(0, 1, 3, 2, 4).reshape(
                owned_count, n_row * tile_rows, n_col * tile_cols
            )

        left_full = squared(
            lax.all_to_all(
                left_edges[:, None], ("row", "col"), split_axis=0, concat_axis=1, tiled=True
            )
        )
        right_full = squared(
            lax.all_to_all(
                right_edges[:, None], ("row", "col"), split_axis=0, concat_axis=1, tiled=True
            )
        )
        equation = "cki,ckj->cij" if update_index == 1 else "cik,cjk->cij"
        products = jnp.einsum(
            equation, left_full, right_full, preferred_element_type=jnp.float32
        )
        returned = return_products(products.astype(jnp.bfloat16))
        gain_out = gains[update_index, 1]
        bias_out = biases[update_index, 1]
        normed_out = layer_norm(
            returned, gain_out[:, None, None], bias_out[:, None, None], 0
        ).astype(jnp.bfloat16)
        mixed = jnp.einsum(
            "cij,cd->ijd", normed_out, w_out[update_index], preferred_element_type=jnp.float32
        )
        gate_vals = jax.nn.sigmoid(
            jnp.dot(
                normed.reshape(tile_rows * tile_cols, channels),
                weights_in[:, 4 * channels : 5 * channels],
                preferred_element_type=jnp.float32,
            ).reshape(tile_rows, tile_cols, channels)
        )
        state = (state.astype(jnp.float32) + gate_vals * mixed).astype(jnp.bfloat16)
    return state


def solution(mesh):
    placed = (P("row", "col", None), P(), P(), P(), P(), P())
    return jax.shard_map(
        body, mesh=mesh, in_specs=placed, out_specs=P("row", "col", None), check_vma=False
    )
```

```python
import functools

import jax
import jax.numpy as jnp
from jax import lax
from jax.experimental import pallas as pl
from jax.experimental.pallas import tpu as pltpu
from jax.sharding import PartitionSpec as P

LANES = 128
HALF = LANES // 2


def layer_norm(values, gain_vec, bias_vec, axis_pos):
    wide = values.astype(jnp.float32)
    average = jnp.mean(wide, axis=axis_pos, keepdims=True)
    centred = wide - average
    variance = jnp.mean(centred * centred, axis=axis_pos, keepdims=True)
    return centred * jax.lax.rsqrt(variance + 1e-05) * gain_vec + bias_vec


def live_values(global_index, chain_lengths, total):
    n_chain = chain_lengths.shape[0]
    slot_size = total // n_chain
    chain_index = global_index // slot_size
    offset = global_index % slot_size
    matches = chain_index[:, None] == jnp.arange(n_chain, dtype=jnp.int32)[None, :]
    live_length = jnp.sum(jnp.where(matches, chain_lengths[None, :], 0), axis=1)
    return (offset < live_length).astype(jnp.float32)


def segments(start, length, tile_cols, n_col):
    runs, at = [], start
    while at < start + length:
        block, inside = divmod(at, tile_cols)
        if inside < LANES:
            stop, packed = block * tile_cols + LANES, block * LANES + inside
        else:
            stop, packed = (block + 1) * tile_cols, n_col * LANES + block * HALF + inside - LANES
        stop = min(stop, start + length)
        runs.append((at - start, packed, stop - at))
        at = stop
    return runs


def join(first, second, upper):
    lanes = slice(HALF, LANES) if upper else slice(0, HALF)
    return jnp.concatenate([first[:, lanes], second[:, lanes]], axis=1)


def triangle_kernel(geometry, incoming, *refs):
    n_row, n_col, rows, cols, first_rows = geometry
    half = rows // 2
    left_first, others, first_out, second_out = refs[:4]
    left, right, tri = refs[4:]
    rest = rows - first_rows
    second_rows = rest + half
    left_parts = (left_first, others.at[:, :, :, :second_rows])
    right_parts = (
        others.at[:, :, :, second_rows:second_rows + first_rows],
        others.at[:, :, :, second_rows + first_rows:],
    )

    def runs_of(r, packed_rows):
        return segments(r * rows, rows, cols, n_col) if packed_rows else [(0, r * rows, rows)]

    def unpack(parts, target, packed_rows):
        first, second = parts
        for r in range(n_row):
            runs = runs_of(r, packed_rows)

            def put(offset, block, lane_at):
                size = block.shape[0]
                for begin, packed, length in runs:
                    lo, hi = max(begin, offset), min(begin + length, offset + size)
                    if lo < hi:
                        target[packed + lo - begin:packed + hi - begin, lane_at:lane_at + LANES] = (
                            block[lo - offset:hi - offset]
                        )

            for s in range(n_col):
                put(0, first[r, s, 0], s * LANES)
                put(first_rows, second[r, s, 0, :rest, :], s * LANES)
            for p in range(n_col // 2):
                even = second[r, 2 * p, 0, rest:, :]
                odd = second[r, 2 * p + 1, 0, rest:, :]
                lane_at = (n_col + p) * LANES
                put(0, join(even, odd, False), lane_at)
                put(half, join(even, odd, True), lane_at)

    unpack(left_parts, left, False)
    unpack(right_parts, right, not incoming)
    contract = ((0,), (0,)) if incoming else ((1,), (1,))
    total = tri.shape[0]
    block = 2 * LANES if total % (2 * LANES) == 0 else LANES

    @pl.loop(0, total // block)
    def _(at):
        span = pl.ds(pl.multiple_of(at * block, block), block)
        lhs = left[:, span] if incoming else left[span, :]
        tri[span, :] = lax.dot_general(
            lhs, right[...], (contract, ((), ())), preferred_element_type=jnp.float32
        ).astype(tri.dtype)

    first, second = first_out, second_out
    for r in range(n_row):
        runs = runs_of(r, incoming)

        def get(offset, size, lane_at):
            pieces = []
            for begin, packed, length in runs:
                lo, hi = max(begin, offset), min(begin + length, offset + size)
                if lo < hi:
                    pieces.append(
                        tri[packed + lo - begin:packed + hi - begin, lane_at:lane_at + LANES]
                    )
            return pieces[0] if len(pieces) == 1 else jnp.concatenate(pieces, axis=0)

        for s in range(n_col):
            first[r, s, 0] = get(0, first_rows, s * LANES)
            second[r, s, 0, :rest, :] = get(first_rows, rest, s * LANES)
        for p in range(n_col // 2):
            lane_at = (n_col + p) * LANES
            above, below = get(0, half, lane_at), get(half, half, lane_at)
            second[r, 2 * p, 0, rest:, :] = join(above, below, False)
            second[r, 2 * p + 1, 0, rest:, :] = join(above, below, True)


def triangle(left_first, others, geometry, incoming):
    n_row, n_col, rows, _, first_rows = geometry
    devices = n_row * n_col
    owned, lanes = left_first.shape[0] // devices, left_first.shape[2]
    total = n_row * rows
    second_rows = rows + rows // 2 - first_rows

    def shape_of(length):
        return (n_row, n_col, owned, length, lanes)

    def spec_of(length):
        return pl.BlockSpec((n_row, n_col, 1, length, lanes), lambda c: (0, 0, c, 0, 0))

    lengths_in, lengths_out = (first_rows, others.shape[1]), (first_rows, second_rows)
    outs = pl.pallas_call(
        functools.partial(triangle_kernel, geometry, incoming),
        grid=(owned,),
        in_specs=[spec_of(length) for length in lengths_in],
        out_specs=[spec_of(length) for length in lengths_out],
        out_shape=[jax.ShapeDtypeStruct(shape_of(length), jnp.bfloat16) for length in lengths_out],
        scratch_shapes=[pltpu.VMEM((total, total), jnp.bfloat16)] * 3,
        cost_estimate=pl.CostEstimate(
            flops=2 * owned * total**3,
            bytes_accessed=3 * (left_first.size + others.size),
            transcendentals=0,
        ),
        compiler_params=pltpu.CompilerParams(vmem_limit_bytes=48 * 2**20),
        name="triangle_in" if incoming else "triangle_out",
    )(left_first.reshape(shape_of(lengths_in[0])), others.reshape(shape_of(lengths_in[1])))
    return [out.reshape(devices * owned, out.shape[3], lanes) for out in outs]


def pack_tile(tile):
    rows, _, channels = tile.shape
    tail = tile[:, LANES:].reshape(2, rows // 2, HALF, channels).transpose(1, 0, 2, 3)
    return jnp.concatenate([tile[:, :LANES], tail.reshape(rows // 2, LANES, channels)], axis=0)


def unpack_tile(packed, rows):
    channels = packed.shape[2]
    tail = packed[rows:].reshape(rows // 2, 2, HALF, channels).transpose(1, 0, 2, 3)
    return jnp.concatenate([packed[:rows], tail.reshape(rows, HALF, channels)], axis=1)


def packed_body(pair, chain_lengths, gains, biases, w_in, w_out):
    tile_rows, tile_cols, channels = pair.shape
    n_row = lax.axis_size("row")
    n_col = lax.axis_size("col")
    first_rows = tile_rows - 16
    geometry = (n_row, n_col, tile_rows, tile_cols, first_rows)
    total = n_row * tile_rows
    row_index = lax.axis_index("row") * tile_rows + jnp.arange(tile_rows, dtype=jnp.int32)
    col_index = lax.axis_index("col") * tile_cols + jnp.arange(tile_cols, dtype=jnp.int32)
    pmask = (
        live_values(row_index, chain_lengths, total)[:, None]
        * live_values(col_index, chain_lengths, total)[None, :]
    )
    pmask = pack_tile(pmask[:, :, None])[:, :, 0]
    masks = [pmask[:first_rows], pmask[first_rows:]]

    def exchange(block):
        return lax.all_to_all(block, ("row", "col"), split_axis=0, concat_axis=0, tiled=True)

    def factor(normed, weights_in, column_block, mask):
        def project(at):
            block = weights_in[:, at * channels : (at + 1) * channels]
            return jnp.einsum("ijc,cd->dij", normed, block, preferred_element_type=jnp.float32)

        gate = jax.nn.sigmoid(project(column_block + 1))
        return (mask[None] * gate * project(column_block)).astype(jnp.bfloat16)

    states = [
        pair[:first_rows, :LANES],
        jnp.concatenate(
            [
                pair[first_rows:, :LANES],
                pair[:, LANES:].reshape(2, tile_rows // 2, HALF, channels)
                .transpose(1, 0, 2, 3)
                .reshape(tile_rows // 2, LANES, channels),
            ],
            axis=0,
        ),
    ]
    for update_index in range(2):
        weights_in = w_in[update_index]
        gain_in, gain_out = gains[update_index, 0], gains[update_index, 1]
        bias_in, bias_out = biases[update_index, 0], biases[update_index, 1]
        normed = [layer_norm(state, gain_in, bias_in, 2).astype(jnp.bfloat16) for state in states]
        left = [factor(n, weights_in, 0, m) for n, m in zip(normed, masks)]
        right = [factor(n, weights_in, 2, m) for n, m in zip(normed, masks)]
        left_first = exchange(left[0])
        others = jnp.concatenate([left[1], right[0], right[1]], axis=1)
        products = triangle(left_first, exchange(others), geometry, update_index == 1)
        returned_first = exchange(products[0])
        returned_first, second = lax.optimization_barrier((returned_first, products[1]))
        later = []
        for state, normed_part, returned in zip(states, normed, (returned_first, exchange(second))):
            normed_out = layer_norm(
                returned, gain_out[:, None, None], bias_out[:, None, None], 0
            ).astype(jnp.bfloat16)
            mixed = jnp.einsum(
                "cij,cd->ijd", normed_out, w_out[update_index], preferred_element_type=jnp.float32
            )
            gate_vals = jax.nn.sigmoid(
                jnp.einsum(
                    "ijc,cd->ijd",
                    normed_part,
                    weights_in[:, 4 * channels : 5 * channels],
                    preferred_element_type=jnp.float32,
                )
            )
            later.append((state.astype(jnp.float32) + gate_vals * mixed).astype(jnp.bfloat16))
        states = later
    return unpack_tile(jnp.concatenate(states, axis=0), tile_rows)


def body(pair, chain_lengths, gains, biases, w_in, w_out):
    tile_rows, tile_cols, channels = pair.shape
    n_row = lax.axis_size("row")
    n_col = lax.axis_size("col")
    if tile_cols == LANES + HALF and tile_rows % 32 == 0 and tile_cols % tile_rows == 0 and n_col % 2 == 0:
        return packed_body(pair, chain_lengths, gains, biases, w_in, w_out)
    owned_count = channels // (n_row * n_col)
    total = n_row * tile_rows
    row_index = lax.axis_index("row") * tile_rows + jnp.arange(tile_rows, dtype=jnp.int32)
    col_index = lax.axis_index("col") * tile_cols + jnp.arange(tile_cols, dtype=jnp.int32)
    pmask = (
        live_values(row_index, chain_lengths, total)[:, None]
        * live_values(col_index, chain_lengths, total)[None, :]
    )

    def return_products(products):
        split = products.reshape(owned_count, n_row, tile_rows, n_col, tile_cols)
        ordered = split.transpose(1, 3, 0, 2, 4).reshape(channels, tile_rows, tile_cols)
        return lax.all_to_all(ordered, ("row", "col"), split_axis=0, concat_axis=0, tiled=True)

    state = pair
    for update_index in range(2):
        weights_in = w_in[update_index]
        normed = layer_norm(state, gains[update_index, 0], biases[update_index, 0], 2).astype(
            jnp.bfloat16
        )

        def project_first(column_block):
            block = weights_in[:, column_block * channels : (column_block + 1) * channels]
            return jnp.einsum("ijc,cd->dij", normed, block, preferred_element_type=jnp.float32)

        left_edges = (pmask[None] * jax.nn.sigmoid(project_first(1)) * project_first(0)).astype(
            jnp.bfloat16
        )
        right_edges = (pmask[None] * jax.nn.sigmoid(project_first(3)) * project_first(2)).astype(
            jnp.bfloat16
        )

        def squared(block):
            split = block.reshape(owned_count, n_row, n_col, tile_rows, tile_cols)
            return split.transpose(0, 1, 3, 2, 4).reshape(
                owned_count, n_row * tile_rows, n_col * tile_cols
            )

        left_full = squared(
            lax.all_to_all(
                left_edges[:, None], ("row", "col"), split_axis=0, concat_axis=1, tiled=True
            )
        )
        right_full = squared(
            lax.all_to_all(
                right_edges[:, None], ("row", "col"), split_axis=0, concat_axis=1, tiled=True
            )
        )
        equation = "cki,ckj->cij" if update_index == 1 else "cik,cjk->cij"
        products = jnp.einsum(
            equation, left_full, right_full, preferred_element_type=jnp.float32
        )
        returned = return_products(products.astype(jnp.bfloat16))
        gain_out = gains[update_index, 1]
        bias_out = biases[update_index, 1]
        normed_out = layer_norm(
            returned, gain_out[:, None, None], bias_out[:, None, None], 0
        ).astype(jnp.bfloat16)
        mixed = jnp.einsum(
            "cij,cd->ijd", normed_out, w_out[update_index], preferred_element_type=jnp.float32
        )
        gate_vals = jax.nn.sigmoid(
            jnp.dot(
                normed.reshape(tile_rows * tile_cols, channels),
                weights_in[:, 4 * channels : 5 * channels],
                preferred_element_type=jnp.float32,
            ).reshape(tile_rows, tile_cols, channels)
        )
        state = (state.astype(jnp.float32) + gate_vals * mixed).astype(jnp.bfloat16)
    return state


def solution(mesh):
    placed = (P("row", "col", None), P(), P(), P(), P(), P())
    return jax.shard_map(
        body, mesh=mesh, in_specs=placed, out_specs=P("row", "col", None), check_vma=False
    )
```

```python
import functools

import jax
import jax.numpy as jnp
from jax import lax
from jax.experimental import pallas as pl
from jax.experimental.pallas import tpu as pltpu
from jax.sharding import PartitionSpec as P

LANES = 128
HALF = LANES // 2


def layer_norm(values, gain_vec, bias_vec, axis_pos):
    wide = values.astype(jnp.float32)
    average = jnp.mean(wide, axis=axis_pos, keepdims=True)
    centred = wide - average
    variance = jnp.mean(centred * centred, axis=axis_pos, keepdims=True)
    return centred * jax.lax.rsqrt(variance + 1e-05) * gain_vec + bias_vec


def live_values(global_index, chain_lengths, total):
    n_chain = chain_lengths.shape[0]
    slot_size = total // n_chain
    chain_index = global_index // slot_size
    offset = global_index % slot_size
    matches = chain_index[:, None] == jnp.arange(n_chain, dtype=jnp.int32)[None, :]
    live_length = jnp.sum(jnp.where(matches, chain_lengths[None, :], 0), axis=1)
    return (offset < live_length).astype(jnp.float32)


def segments(start, length, tile_cols, n_col):
    runs, at = [], start
    while at < start + length:
        block, inside = divmod(at, tile_cols)
        if inside < LANES:
            stop, packed = block * tile_cols + LANES, block * LANES + inside
        else:
            stop, packed = (block + 1) * tile_cols, n_col * LANES + block * HALF + inside - LANES
        stop = min(stop, start + length)
        runs.append((at - start, packed, stop - at))
        at = stop
    return runs


def join(first, second, upper):
    lanes = slice(HALF, LANES) if upper else slice(0, HALF)
    return jnp.concatenate([first[:, lanes], second[:, lanes]], axis=1)


def triangle_kernel(geometry, incoming, *refs):
    n_row, n_col, rows, cols, first_rows = geometry
    half = rows // 2
    left_first, others, first_out, second_out = refs[:4]
    left, right, tri = refs[4:]
    rest = rows - first_rows
    second_rows = rest + half
    left_parts = (left_first, others.at[:, :, :, :second_rows])
    right_parts = (
        others.at[:, :, :, second_rows:second_rows + first_rows],
        others.at[:, :, :, second_rows + first_rows:],
    )

    def runs_of(r, packed_rows):
        return segments(r * rows, rows, cols, n_col) if packed_rows else [(0, r * rows, rows)]

    def unpack(parts, target, packed_rows):
        first, second = parts
        for r in range(n_row):
            runs = runs_of(r, packed_rows)

            def put(offset, block, lane_at):
                size = block.shape[0]
                for begin, packed, length in runs:
                    lo, hi = max(begin, offset), min(begin + length, offset + size)
                    if lo < hi:
                        target[packed + lo - begin:packed + hi - begin, lane_at:lane_at + LANES] = (
                            block[lo - offset:hi - offset]
                        )

            for s in range(n_col):
                put(0, first[r, s, 0], s * LANES)
                put(first_rows, second[r, s, 0, :rest, :], s * LANES)
            for p in range(n_col // 2):
                even = second[r, 2 * p, 0, rest:, :]
                odd = second[r, 2 * p + 1, 0, rest:, :]
                lane_at = (n_col + p) * LANES
                put(0, join(even, odd, False), lane_at)
                put(half, join(even, odd, True), lane_at)

    unpack(left_parts, left, False)
    unpack(right_parts, right, not incoming)
    contract = ((0,), (0,)) if incoming else ((1,), (1,))
    tri[...] = lax.dot_general(
        left[...], right[...], (contract, ((), ())), preferred_element_type=jnp.float32
    ).astype(tri.dtype)

    first, second = first_out, second_out
    for r in range(n_row):
        runs = runs_of(r, incoming)

        def get(offset, size, lane_at):
            pieces = []
            for begin, packed, length in runs:
                lo, hi = max(begin, offset), min(begin + length, offset + size)
                if lo < hi:
                    pieces.append(
                        tri[packed + lo - begin:packed + hi - begin, lane_at:lane_at + LANES]
                    )
            return pieces[0] if len(pieces) == 1 else jnp.concatenate(pieces, axis=0)

        for s in range(n_col):
            first[r, s, 0] = get(0, first_rows, s * LANES)
            second[r, s, 0, :rest, :] = get(first_rows, rest, s * LANES)
        for p in range(n_col // 2):
            lane_at = (n_col + p) * LANES
            above, below = get(0, half, lane_at), get(half, half, lane_at)
            second[r, 2 * p, 0, rest:, :] = join(above, below, False)
            second[r, 2 * p + 1, 0, rest:, :] = join(above, below, True)


def triangle(left_first, others, geometry, incoming):
    n_row, n_col, rows, _, first_rows = geometry
    devices = n_row * n_col
    owned, lanes = left_first.shape[0] // devices, left_first.shape[2]
    total = n_row * rows
    second_rows = rows + rows // 2 - first_rows

    def shape_of(length):
        return (n_row, n_col, owned, length, lanes)

    def spec_of(length):
        return pl.BlockSpec((n_row, n_col, 1, length, lanes), lambda c: (0, 0, c, 0, 0))

    lengths_in, lengths_out = (first_rows, others.shape[1]), (first_rows, second_rows)
    outs = pl.pallas_call(
        functools.partial(triangle_kernel, geometry, incoming),
        grid=(owned,),
        in_specs=[spec_of(length) for length in lengths_in],
        out_specs=[spec_of(length) for length in lengths_out],
        out_shape=[jax.ShapeDtypeStruct(shape_of(length), jnp.bfloat16) for length in lengths_out],
        scratch_shapes=[pltpu.VMEM((total, total), jnp.bfloat16)] * 3,
        cost_estimate=pl.CostEstimate(
            flops=2 * owned * total**3,
            bytes_accessed=3 * (left_first.size + others.size),
            transcendentals=0,
        ),
        compiler_params=pltpu.CompilerParams(vmem_limit_bytes=48 * 2**20),
        name="triangle_in" if incoming else "triangle_out",
    )(left_first.reshape(shape_of(lengths_in[0])), others.reshape(shape_of(lengths_in[1])))
    return [out.reshape(devices * owned, out.shape[3], lanes) for out in outs]


def pack_tile(tile):
    rows, _, channels = tile.shape
    tail = tile[:, LANES:].reshape(2, rows // 2, HALF, channels).transpose(1, 0, 2, 3)
    return jnp.concatenate([tile[:, :LANES], tail.reshape(rows // 2, LANES, channels)], axis=0)


def unpack_tile(packed, rows):
    channels = packed.shape[2]
    tail = packed[rows:].reshape(rows // 2, 2, HALF, channels).transpose(1, 0, 2, 3)
    return jnp.concatenate([packed[:rows], tail.reshape(rows, HALF, channels)], axis=1)


def packed_body(pair, chain_lengths, gains, biases, w_in, w_out):
    tile_rows, tile_cols, channels = pair.shape
    n_row = lax.axis_size("row")
    n_col = lax.axis_size("col")
    first_rows = tile_rows - 16
    geometry = (n_row, n_col, tile_rows, tile_cols, first_rows)
    total = n_row * tile_rows
    row_index = lax.axis_index("row") * tile_rows + jnp.arange(tile_rows, dtype=jnp.int32)
    col_index = lax.axis_index("col") * tile_cols + jnp.arange(tile_cols, dtype=jnp.int32)
    pmask = (
        live_values(row_index, chain_lengths, total)[:, None]
        * live_values(col_index, chain_lengths, total)[None, :]
    )
    pmask = pack_tile(pmask[:, :, None])[:, :, 0]
    masks = [pmask[:first_rows], pmask[first_rows:]]

    def exchange(block):
        return lax.all_to_all(block, ("row", "col"), split_axis=0, concat_axis=0, tiled=True)

    def factor(normed, weights_in, column_block, mask):
        def project(at):
            block = weights_in[:, at * channels : (at + 1) * channels]
            return jnp.einsum("ijc,cd->dij", normed, block, preferred_element_type=jnp.float32)

        gate = jax.nn.sigmoid(project(column_block + 1))
        return (mask[None] * gate * project(column_block)).astype(jnp.bfloat16)

    states = [
        pair[:first_rows, :LANES],
        jnp.concatenate(
            [
                pair[first_rows:, :LANES],
                pair[:, LANES:].reshape(2, tile_rows // 2, HALF, channels)
                .transpose(1, 0, 2, 3)
                .reshape(tile_rows // 2, LANES, channels),
            ],
            axis=0,
        ),
    ]
    for update_index in range(2):
        weights_in = w_in[update_index]
        gain_in, gain_out = gains[update_index, 0], gains[update_index, 1]
        bias_in, bias_out = biases[update_index, 0], biases[update_index, 1]
        normed = [layer_norm(state, gain_in, bias_in, 2).astype(jnp.bfloat16) for state in states]
        left = [factor(n, weights_in, 0, m) for n, m in zip(normed, masks)]
        right = [factor(n, weights_in, 2, m) for n, m in zip(normed, masks)]
        left_first = exchange(left[0])
        others = jnp.concatenate([left[1], right[0], right[1]], axis=1)
        products = triangle(left_first, exchange(others), geometry, update_index == 1)
        returned_first = exchange(products[0])
        returned_first, second = lax.optimization_barrier((returned_first, products[1]))
        later = []
        for state, normed_part, returned in zip(states, normed, (returned_first, exchange(second))):
            normed_out = layer_norm(
                returned, gain_out[:, None, None], bias_out[:, None, None], 0
            ).astype(jnp.bfloat16)
            mixed = jnp.einsum(
                "cij,cd->ijd", normed_out, w_out[update_index], preferred_element_type=jnp.float32
            )
            gate_vals = jax.nn.sigmoid(
                jnp.einsum(
                    "ijc,cd->ijd",
                    normed_part,
                    weights_in[:, 4 * channels : 5 * channels],
                    preferred_element_type=jnp.float32,
                )
            )
            later.append((state.astype(jnp.float32) + gate_vals * mixed).astype(jnp.bfloat16))
        states = later
    return unpack_tile(jnp.concatenate(states, axis=0), tile_rows)


def body(pair, chain_lengths, gains, biases, w_in, w_out):
    tile_rows, tile_cols, channels = pair.shape
    n_row = lax.axis_size("row")
    n_col = lax.axis_size("col")
    if tile_cols == LANES + HALF and tile_rows % 32 == 0 and tile_cols % tile_rows == 0 and n_col % 2 == 0:
        return packed_body(pair, chain_lengths, gains, biases, w_in, w_out)
    owned_count = channels // (n_row * n_col)
    total = n_row * tile_rows
    row_index = lax.axis_index("row") * tile_rows + jnp.arange(tile_rows, dtype=jnp.int32)
    col_index = lax.axis_index("col") * tile_cols + jnp.arange(tile_cols, dtype=jnp.int32)
    pmask = (
        live_values(row_index, chain_lengths, total)[:, None]
        * live_values(col_index, chain_lengths, total)[None, :]
    )

    def return_products(products):
        split = products.reshape(owned_count, n_row, tile_rows, n_col, tile_cols)
        ordered = split.transpose(1, 3, 0, 2, 4).reshape(channels, tile_rows, tile_cols)
        return lax.all_to_all(ordered, ("row", "col"), split_axis=0, concat_axis=0, tiled=True)

    state = pair
    for update_index in range(2):
        weights_in = w_in[update_index]
        normed = layer_norm(state, gains[update_index, 0], biases[update_index, 0], 2).astype(
            jnp.bfloat16
        )

        def project_first(column_block):
            block = weights_in[:, column_block * channels : (column_block + 1) * channels]
            return jnp.einsum("ijc,cd->dij", normed, block, preferred_element_type=jnp.float32)

        left_edges = (pmask[None] * jax.nn.sigmoid(project_first(1)) * project_first(0)).astype(
            jnp.bfloat16
        )
        right_edges = (pmask[None] * jax.nn.sigmoid(project_first(3)) * project_first(2)).astype(
            jnp.bfloat16
        )

        def squared(block):
            split = block.reshape(owned_count, n_row, n_col, tile_rows, tile_cols)
            return split.transpose(0, 1, 3, 2, 4).reshape(
                owned_count, n_row * tile_rows, n_col * tile_cols
            )

        left_full = squared(
            lax.all_to_all(
                left_edges[:, None], ("row", "col"), split_axis=0, concat_axis=1, tiled=True
            )
        )
        right_full = squared(
            lax.all_to_all(
                right_edges[:, None], ("row", "col"), split_axis=0, concat_axis=1, tiled=True
            )
        )
        equation = "cki,ckj->cij" if update_index == 1 else "cik,cjk->cij"
        products = jnp.einsum(
            equation, left_full, right_full, preferred_element_type=jnp.float32
        )
        returned = return_products(products.astype(jnp.bfloat16))
        gain_out = gains[update_index, 1]
        bias_out = biases[update_index, 1]
        normed_out = layer_norm(
            returned, gain_out[:, None, None], bias_out[:, None, None], 0
        ).astype(jnp.bfloat16)
        mixed = jnp.einsum(
            "cij,cd->ijd", normed_out, w_out[update_index], preferred_element_type=jnp.float32
        )
        gate_vals = jax.nn.sigmoid(
            jnp.dot(
                normed.reshape(tile_rows * tile_cols, channels),
                weights_in[:, 4 * channels : 5 * channels],
                preferred_element_type=jnp.float32,
            ).reshape(tile_rows, tile_cols, channels)
        )
        state = (state.astype(jnp.float32) + gate_vals * mixed).astype(jnp.bfloat16)
    return state


def solution(mesh):
    placed = (P("row", "col", None), P(), P(), P(), P(), P())
    return jax.shard_map(
        body, mesh=mesh, in_specs=placed, out_specs=P("row", "col", None), check_vma=False
    )
```

```python
import functools

import jax
import jax.numpy as jnp
from jax import lax
from jax.experimental import pallas as pl
from jax.experimental.pallas import tpu as pltpu
from jax.sharding import PartitionSpec as P

LANES = 128
HALF = LANES // 2


def layer_norm(values, gain_vec, bias_vec, axis_pos):
    wide = values.astype(jnp.float32)
    average = jnp.mean(wide, axis=axis_pos, keepdims=True)
    centred = wide - average
    variance = jnp.mean(centred * centred, axis=axis_pos, keepdims=True)
    return centred * jax.lax.rsqrt(variance + 1e-05) * gain_vec + bias_vec


def live_values(global_index, chain_lengths, total):
    n_chain = chain_lengths.shape[0]
    slot_size = total // n_chain
    chain_index = global_index // slot_size
    offset = global_index % slot_size
    matches = chain_index[:, None] == jnp.arange(n_chain, dtype=jnp.int32)[None, :]
    live_length = jnp.sum(jnp.where(matches, chain_lengths[None, :], 0), axis=1)
    return (offset < live_length).astype(jnp.float32)


def segments(start, length, tile_cols, n_col):
    runs, at = [], start
    while at < start + length:
        block, inside = divmod(at, tile_cols)
        if inside < LANES:
            stop, packed = block * tile_cols + LANES, block * LANES + inside
        else:
            stop, packed = (block + 1) * tile_cols, n_col * LANES + block * HALF + inside - LANES
        stop = min(stop, start + length)
        runs.append((at - start, packed, stop - at))
        at = stop
    return runs


def join(first, second, upper):
    lanes = slice(HALF, LANES) if upper else slice(0, HALF)
    return jnp.concatenate([first[:, lanes], second[:, lanes]], axis=1)


def triangle_kernel(geometry, incoming, *refs):
    n_row, n_col, rows, cols, first_rows = geometry
    half = rows // 2
    left_first, others, first_out, second_out = refs[:4]
    left, right, tri = refs[4:]
    rest = rows - first_rows
    second_rows = rest + half
    left_parts = (left_first, others.at[:, :, :, :second_rows])
    right_parts = (
        others.at[:, :, :, second_rows:second_rows + first_rows],
        others.at[:, :, :, second_rows + first_rows:],
    )

    def runs_of(r, packed_rows):
        return segments(r * rows, rows, cols, n_col) if packed_rows else [(0, r * rows, rows)]

    def unpack(parts, target, packed_rows):
        first, second = parts
        for r in range(n_row):
            runs = runs_of(r, packed_rows)

            def put(offset, block, lane_at):
                size = block.shape[0]
                for begin, packed, length in runs:
                    lo, hi = max(begin, offset), min(begin + length, offset + size)
                    if lo < hi:
                        target[packed + lo - begin:packed + hi - begin, lane_at:lane_at + LANES] = (
                            block[lo - offset:hi - offset]
                        )

            for s in range(n_col):
                put(0, first[r, s, 0], s * LANES)
                put(first_rows, second[r, s, 0, :rest, :], s * LANES)
            for p in range(n_col // 2):
                even = second[r, 2 * p, 0, rest:, :]
                odd = second[r, 2 * p + 1, 0, rest:, :]
                lane_at = (n_col + p) * LANES
                put(0, join(even, odd, False), lane_at)
                put(half, join(even, odd, True), lane_at)

    unpack(left_parts, left, False)
    unpack(right_parts, right, not incoming)
    contract = ((0,), (0,)) if incoming else ((1,), (1,))
    tri[...] = lax.dot_general(
        left[...], right[...], (contract, ((), ())), preferred_element_type=jnp.float32
    ).astype(tri.dtype)

    first, second = first_out, second_out
    for r in range(n_row):
        runs = runs_of(r, incoming)

        def get(offset, size, lane_at):
            pieces = []
            for begin, packed, length in runs:
                lo, hi = max(begin, offset), min(begin + length, offset + size)
                if lo < hi:
                    pieces.append(
                        tri[packed + lo - begin:packed + hi - begin, lane_at:lane_at + LANES]
                    )
            return pieces[0] if len(pieces) == 1 else jnp.concatenate(pieces, axis=0)

        for s in range(n_col):
            first[r, s, 0] = get(0, first_rows, s * LANES)
            second[r, s, 0, :rest, :] = get(first_rows, rest, s * LANES)
        for p in range(n_col // 2):
            lane_at = (n_col + p) * LANES
            above, below = get(0, half, lane_at), get(half, half, lane_at)
            second[r, 2 * p, 0, rest:, :] = join(above, below, False)
            second[r, 2 * p + 1, 0, rest:, :] = join(above, below, True)


def triangle(left_first, others, geometry, incoming):
    n_row, n_col, rows, _, first_rows = geometry
    devices = n_row * n_col
    owned, lanes = left_first.shape[0] // devices, left_first.shape[2]
    total = n_row * rows
    second_rows = rows + rows // 2 - first_rows

    def shape_of(length):
        return (n_row, n_col, owned, length, lanes)

    def spec_of(length):
        return pl.BlockSpec((n_row, n_col, 1, length, lanes), lambda c: (0, 0, c, 0, 0))

    lengths_in, lengths_out = (first_rows, others.shape[1]), (first_rows, second_rows)
    outs = pl.pallas_call(
        functools.partial(triangle_kernel, geometry, incoming),
        grid=(owned,),
        in_specs=[spec_of(length) for length in lengths_in],
        out_specs=[spec_of(length) for length in lengths_out],
        out_shape=[jax.ShapeDtypeStruct(shape_of(length), jnp.bfloat16) for length in lengths_out],
        scratch_shapes=[pltpu.VMEM((total, total), jnp.bfloat16)] * 3,
        cost_estimate=pl.CostEstimate(
            flops=2 * owned * total**3,
            bytes_accessed=3 * (left_first.size + others.size),
            transcendentals=0,
        ),
        compiler_params=pltpu.CompilerParams(vmem_limit_bytes=48 * 2**20),
        name="triangle_in" if incoming else "triangle_out",
    )(left_first.reshape(shape_of(lengths_in[0])), others.reshape(shape_of(lengths_in[1])))
    return [out.reshape(devices * owned, out.shape[3], lanes) for out in outs]


def pack_tile(tile):
    rows, _, channels = tile.shape
    tail = tile[:, LANES:].reshape(2, rows // 2, HALF, channels).transpose(1, 0, 2, 3)
    return jnp.concatenate([tile[:, :LANES], tail.reshape(rows // 2, LANES, channels)], axis=0)


def unpack_tile(packed, rows):
    channels = packed.shape[2]
    tail = packed[rows:].reshape(rows // 2, 2, HALF, channels).transpose(1, 0, 2, 3)
    return jnp.concatenate([packed[:rows], tail.reshape(rows, HALF, channels)], axis=1)


def packed_body(pair, chain_lengths, gains, biases, w_in, w_out):
    tile_rows, tile_cols, channels = pair.shape
    n_row = lax.axis_size("row")
    n_col = lax.axis_size("col")
    first_rows = tile_rows - 16
    geometry = (n_row, n_col, tile_rows, tile_cols, first_rows)
    total = n_row * tile_rows
    row_index = lax.axis_index("row") * tile_rows + jnp.arange(tile_rows, dtype=jnp.int32)
    col_index = lax.axis_index("col") * tile_cols + jnp.arange(tile_cols, dtype=jnp.int32)
    pmask = (
        live_values(row_index, chain_lengths, total)[:, None]
        * live_values(col_index, chain_lengths, total)[None, :]
    )
    pmask = pack_tile(pmask[:, :, None])[:, :, 0]
    masks = [pmask[:first_rows], pmask[first_rows:]]

    def exchange(block):
        return lax.all_to_all(block, ("row", "col"), split_axis=0, concat_axis=0, tiled=True)

    def factor(normed, weights_in, column_block, mask):
        def project(at):
            block = weights_in[:, at * channels : (at + 1) * channels]
            return jnp.einsum("ijc,cd->dij", normed, block, preferred_element_type=jnp.float32)

        gate = jax.nn.sigmoid(project(column_block + 1))
        return (mask[None] * gate * project(column_block)).astype(jnp.bfloat16)

    states = [
        pair[:first_rows, :LANES],
        jnp.concatenate(
            [
                pair[first_rows:, :LANES],
                pair[:, LANES:].reshape(2, tile_rows // 2, HALF, channels)
                .transpose(1, 0, 2, 3)
                .reshape(tile_rows // 2, LANES, channels),
            ],
            axis=0,
        ),
    ]
    for update_index in range(2):
        weights_in = w_in[update_index]
        gain_in, gain_out = gains[update_index, 0], gains[update_index, 1]
        bias_in, bias_out = biases[update_index, 0], biases[update_index, 1]
        normed = [layer_norm(state, gain_in, bias_in, 2).astype(jnp.bfloat16) for state in states]
        left = [factor(n, weights_in, 0, m) for n, m in zip(normed, masks)]
        right = [factor(n, weights_in, 2, m) for n, m in zip(normed, masks)]
        left_first = exchange(left[0])
        others = jnp.concatenate([left[1], right[0], right[1]], axis=1)
        products = triangle(left_first, exchange(others), geometry, update_index == 1)
        lead = update_index
        leading = exchange(products[lead])
        leading, other = lax.optimization_barrier((leading, products[1 - lead]))
        arrived = [leading, exchange(other)]
        if lead == 1:
            arrived.reverse()
        later = []
        for state, normed_part, returned in zip(states, normed, arrived):
            normed_out = layer_norm(
                returned, gain_out[:, None, None], bias_out[:, None, None], 0
            ).astype(jnp.bfloat16)
            mixed = jnp.einsum(
                "cij,cd->ijd", normed_out, w_out[update_index], preferred_element_type=jnp.float32
            )
            gate_vals = jax.nn.sigmoid(
                jnp.einsum(
                    "ijc,cd->ijd",
                    normed_part,
                    weights_in[:, 4 * channels : 5 * channels],
                    preferred_element_type=jnp.float32,
                )
            )
            later.append((state.astype(jnp.float32) + gate_vals * mixed).astype(jnp.bfloat16))
        states = later
    return unpack_tile(jnp.concatenate(states, axis=0), tile_rows)


def body(pair, chain_lengths, gains, biases, w_in, w_out):
    tile_rows, tile_cols, channels = pair.shape
    n_row = lax.axis_size("row")
    n_col = lax.axis_size("col")
    if tile_cols == LANES + HALF and tile_rows % 32 == 0 and tile_cols % tile_rows == 0 and n_col % 2 == 0:
        return packed_body(pair, chain_lengths, gains, biases, w_in, w_out)
    owned_count = channels // (n_row * n_col)
    total = n_row * tile_rows
    row_index = lax.axis_index("row") * tile_rows + jnp.arange(tile_rows, dtype=jnp.int32)
    col_index = lax.axis_index("col") * tile_cols + jnp.arange(tile_cols, dtype=jnp.int32)
    pmask = (
        live_values(row_index, chain_lengths, total)[:, None]
        * live_values(col_index, chain_lengths, total)[None, :]
    )

    def return_products(products):
        split = products.reshape(owned_count, n_row, tile_rows, n_col, tile_cols)
        ordered = split.transpose(1, 3, 0, 2, 4).reshape(channels, tile_rows, tile_cols)
        return lax.all_to_all(ordered, ("row", "col"), split_axis=0, concat_axis=0, tiled=True)

    state = pair
    for update_index in range(2):
        weights_in = w_in[update_index]
        normed = layer_norm(state, gains[update_index, 0], biases[update_index, 0], 2).astype(
            jnp.bfloat16
        )

        def project_first(column_block):
            block = weights_in[:, column_block * channels : (column_block + 1) * channels]
            return jnp.einsum("ijc,cd->dij", normed, block, preferred_element_type=jnp.float32)

        left_edges = (pmask[None] * jax.nn.sigmoid(project_first(1)) * project_first(0)).astype(
            jnp.bfloat16
        )
        right_edges = (pmask[None] * jax.nn.sigmoid(project_first(3)) * project_first(2)).astype(
            jnp.bfloat16
        )

        def squared(block):
            split = block.reshape(owned_count, n_row, n_col, tile_rows, tile_cols)
            return split.transpose(0, 1, 3, 2, 4).reshape(
                owned_count, n_row * tile_rows, n_col * tile_cols
            )

        left_full = squared(
            lax.all_to_all(
                left_edges[:, None], ("row", "col"), split_axis=0, concat_axis=1, tiled=True
            )
        )
        right_full = squared(
            lax.all_to_all(
                right_edges[:, None], ("row", "col"), split_axis=0, concat_axis=1, tiled=True
            )
        )
        equation = "cki,ckj->cij" if update_index == 1 else "cik,cjk->cij"
        products = jnp.einsum(
            equation, left_full, right_full, preferred_element_type=jnp.float32
        )
        returned = return_products(products.astype(jnp.bfloat16))
        gain_out = gains[update_index, 1]
        bias_out = biases[update_index, 1]
        normed_out = layer_norm(
            returned, gain_out[:, None, None], bias_out[:, None, None], 0
        ).astype(jnp.bfloat16)
        mixed = jnp.einsum(
            "cij,cd->ijd", normed_out, w_out[update_index], preferred_element_type=jnp.float32
        )
        gate_vals = jax.nn.sigmoid(
            jnp.dot(
                normed.reshape(tile_rows * tile_cols, channels),
                weights_in[:, 4 * channels : 5 * channels],
                preferred_element_type=jnp.float32,
            ).reshape(tile_rows, tile_cols, channels)
        )
        state = (state.astype(jnp.float32) + gate_vals * mixed).astype(jnp.bfloat16)
    return state


def solution(mesh):
    placed = (P("row", "col", None), P(), P(), P(), P(), P())
    return jax.shard_map(
        body, mesh=mesh, in_specs=placed, out_specs=P("row", "col", None), check_vma=False
    )
```
